512 devices in a mesh: row: 32 (over y, x), col: 16 (over z, core).
Axes of the slice: x: 4, y: 8, z: 8, core: 2. Of those that a mesh axis runs over, the one named last changes fastest.
Arguments:
- draws: bfloat16 [128, 65536], P('row', 'col'), may hold values from -6 to 6
- u_factors: bfloat16 [64, 64, 1024, 64], P('row', 'col'), may hold values from -0.09375 to 0.09375
- v_factors: bfloat16 [64, 64, 1024, 64], P('row', 'col'), may hold values from -0.1875 to 0.1875
- ranks: int32 [64, 64], P('row', 'col'), may hold values from 16 to 64
- near: int32 [64, 16], P('row'), may hold values from 0 to 63, as said below
- row_coords: float32 [2, 65536], P(None, 'row'), may hold values from 0 to 16
- col_coords: float32 [2, 65536], replicated, may hold values from 0 to 16
Outputs:
- applied: float32 [128, 65536], P('col', 'row')
The draws below stay inside these ranges and needn't reach their ends.
Inputs may be any that keep to these rules, and one draw needn't show every extreme that they name: `ranks`: the rank of a tile; factor columns from its rank on are padding. `near`: each block row lists 16 different block columns.
All inputs are finite; a program needn't handle non-finite values.
Results may differ from the reference program's by a relative error of at most 0.0029.
Values may be sent and summed in bfloat16 or wider, within the bound.
No kernel may reach another device: no remote copies, remote signals or barrier semaphores. Data moves between devices by JAX's collectives and lax.ppermute only.
A program may use at most 64 MiB of HBM per device.

```python
import jax
import jax.numpy as jnp
from jax import lax

TILE = 1024
RANK = 64
NRHS = 128
NEAR = 16
BR = 64
BC = 64


def cell_place(index):
    column = index // 4
    within = index % 4
    upward = jnp.where(column % 2 == 0, within, 3 - within)
    return (column, upward)


def row_cells(key):
    first, second, third, fourth = jax.random.split(key, 4)
    spot = jax.random.randint(first, (), 0, BC)
    beside_all = jax.random.randint(second, (BR,), 0, min(12, BC))
    spread = jax.random.randint(third, (BR,), 0, BC)
    pick = jax.random.randint(fourth, (BR,), 0, 2)
    return jnp.where(pick == 1, (spot + beside_all) % BC, spread).astype(jnp.int32)


def draw_near(key, part):
    cells = row_cells(jax.random.fold_in(key, 7))
    row_x, row_y = cell_place(cells)
    column_ids = jnp.arange(BC, dtype=jnp.int32)
    col_x, col_y = cell_place(column_ids)
    delta_x = row_x[:, None] - col_x[None, :]
    delta_y = row_y[:, None] - col_y[None, :]
    squared = delta_x * delta_x + delta_y * delta_y
    offset = jax.random.randint(jax.random.fold_in(key, 9), (BR, 1), 0, BC)
    score = squared * BC + (column_ids[None, :] + offset) % BC
    values, picked = lax.top_k(-score, NEAR)
    return picked.astype(jnp.int32)


def draw_row_coords(key, part):
    cells = row_cells(jax.random.fold_in(key, 7))
    site_cells = jnp.repeat(cells, TILE)
    cell_x, cell_y = cell_place(site_cells)
    jitter = jax.random.uniform(jax.random.fold_in(key, 13), (2, BR * TILE), jnp.float32)
    return jnp.stack([cell_x, cell_y]).astype(jnp.float32) + jitter


def draw_col_coords(key, part):
    site_cells = jnp.arange(BC * TILE, dtype=jnp.int32) // TILE
    cell_x, cell_y = cell_place(site_cells)
    jitter = jax.random.uniform(jax.random.fold_in(key, 11), (2, BC * TILE), jnp.float32)
    return jnp.stack([cell_x, cell_y]).astype(jnp.float32) + jitter


def plant(array, stream_key, low, top_value):
    longest = array.shape.index(max(array.shape))
    spots = []
    for shift in (0, 1):
        where = [jax.random.randint(jax.random.fold_in(stream_key, axis), (), 0, length) for axis, length in enumerate(array.shape)]
        where[longest] = (where[longest] + shift) % array.shape[longest]
        spots.append(tuple(where))
    return array.at[spots[0]].set(low).at[spots[1]].set(top_value)


def level_of(own_key, extent, pieces, low, largest):
    def one(axis_at, shards_of):
        steps = jax.random.uniform(jax.random.fold_in(jax.random.fold_in(own_key, 6), axis_at), (shards_of,), jnp.float32, low / len(pieces), largest / len(pieces))
        return jnp.repeat(jnp.exp(steps), extent[axis_at] // shards_of).reshape((-1,) + (1,) * (len(extent) - axis_at - 1))

    factor_of = one(*pieces[0])
    for cut in pieces[1:]:
        factor_of = factor_of * one(*cut)
    return factor_of


def normal_values(own_key, shape, deviation, most, cuts=(), kind=jnp.bfloat16):
    loudness = level_of(own_key, shape, cuts, -0.22, 0.18) if cuts else 1.0
    drawn = jax.random.normal(own_key, shape, jnp.float32) * deviation * loudness
    return jnp.minimum(jnp.maximum(drawn, -most), most).astype(kind)


def setup_inputs(seed: int = 0) -> dict:
    keys = jax.random.split(jax.random.key(seed), 8)
    draws = normal_values(keys[0], (NRHS, BC * TILE), 1.0, 6.0, ((0, 32), (1, 16)))
    u_factors = normal_values(keys[1], (BR, BC, TILE, RANK), (RANK * BC) ** -0.5, 0.09375, ((0, 32), (1, 16)))
    v_factors = normal_values(keys[2], (BR, BC, TILE, RANK), TILE ** -0.5, 0.1875, ((0, 32), (1, 16)))
    ranks = plant(jax.random.randint(keys[3], (BR, BC), RANK // 4, RANK + 1), jax.random.fold_in(keys[3], 1), RANK // 4, RANK).astype(jnp.int32)
    near = draw_near(jax.random.fold_in(keys[7], 71), 0)
    row_coords = draw_row_coords(jax.random.fold_in(keys[7], 71), 0)
    col_coords = draw_col_coords(jax.random.fold_in(keys[7], 71), 0)
    return {"draws": draws, "u_factors": u_factors, "v_factors": v_factors, "ranks": ranks, "near": near, "row_coords": row_coords, "col_coords": col_coords}


def matern_tile(col_part, row_part):
    delta_x = col_part[0][:, None] - row_part[0][None, :]
    delta_y = col_part[1][:, None] - row_part[1][None, :]
    kernel = jnp.exp(-jnp.sqrt(delta_x * delta_x + delta_y * delta_y)) * 0.03125
    return kernel.astype(jnp.bfloat16)

def reference(draws, u_factors, v_factors, ranks, near, row_coords, col_coords):
    blocks = draws.reshape(NRHS, BC, TILE).astype(jnp.float32)
    column_ids = jnp.arange(BC, dtype=jnp.int32)
    flagged = jnp.any(near[:, :, None] == column_ids[None, None, :], axis=1)
    rank_ids = jnp.arange(RANK, dtype=jnp.int32)

    def one_row(index):
        v_row = v_factors[index].astype(jnp.float32)
        u_row = u_factors[index].astype(jnp.float32)
        reduced = jnp.einsum('nbt,btk->nbk', blocks, v_row)
        keep = (rank_ids[None, :] < ranks[index][:, None]) & jnp.logical_not(flagged[index])[:, None]
        reduced = jnp.where(keep[None], reduced, 0.0).astype(jnp.bfloat16).astype(jnp.float32)
        total = jnp.einsum('nbk,btk->nt', reduced, u_row)
        row_part = lax.dynamic_slice_in_dim(row_coords, (index * TILE).astype(jnp.int32), TILE, 1)

        def add_slot(slot, acc):
            column = near[index, slot].astype(jnp.int32)
            tile_matrix = matern_tile(lax.dynamic_slice_in_dim(col_coords, column * TILE, TILE, 1), row_part)
            piece = lax.dynamic_slice_in_dim(draws, column * TILE, TILE, 1)
            return acc + jnp.dot(piece, tile_matrix, preferred_element_type=jnp.float32)
        return lax.fori_loop(0, NEAR, add_slot, total)
    rows_out = lax.map(one_row, jnp.arange(BR, dtype=jnp.int32))
    return jnp.transpose(rows_out, (1, 0, 2)).reshape(NRHS, BR * TILE)
```

```python
import functools

import jax
import jax.numpy as jnp
from jax import lax
from jax.experimental import pallas as pl
from jax.experimental.pallas import tpu as pltpu
from jax.sharding import Mesh, PartitionSpec as P

LOG2E = 1.4426950408889634
AXES = ("y", "x", "z", "c")
SIZES = (8, 4, 8, 2)
VMEM = pltpu.MemorySpace.VMEM
SMEM = pltpu.MemorySpace.SMEM
HBM = pltpu.MemorySpace.HBM


def first_column(cols_local):
    return (lax.axis_index("z") * 2 + lax.axis_index("c")) * cols_local


def is_near(near_ref, row, column):
    hit = near_ref[row, 0] == column
    for slot in range(1, near_ref.shape[1]):
        hit = jnp.logical_or(hit, near_ref[row, slot] == column)
    return hit


def dense_kernel(near_ref, row_ref, col_hbm, out_hbm, coords, wide_x, wide_y, block, todo, sem, out_sems):
    rows_local, cols_local, tile, _ = out_hbm.shape
    first = first_column(cols_local)
    start = pl.multiple_of(first * tile, tile)
    fetch = pltpu.make_async_copy(col_hbm.at[:, pl.ds(start, cols_local * tile)], coords, sem)
    fetch.start()
    count = jnp.int32(0)
    for b in range(cols_local):
        for a in range(rows_local):
            todo[count] = b * rows_local + a
            count = count + is_near(near_ref, a, first + b).astype(jnp.int32)
    fetch.wait()
    step = 32

    def store(index):
        a, b, slot = lax.rem(todo[index], rows_local), lax.div(todo[index], rows_local), lax.rem(index, 2)
        return pltpu.make_async_copy(block.at[slot], out_hbm.at[a, b], out_sems.at[slot])

    def make_tile(index, carry):
        a, b, slot = lax.rem(todo[index], rows_local), lax.div(todo[index], rows_local), lax.rem(index, 2)

        @pl.when(index >= 2)
        def _():
            store(index - 2).wait()

        for part in range(tile // 128):
            at = pl.multiple_of(b * tile + part * 128, 128)
            for axis, wide in ((0, wide_x), (1, wide_y)):
                line = coords[axis : axis + 1, pl.ds(at, 128)] * LOG2E
                wide[part * 128 : (part + 1) * 128, :] = jnp.broadcast_to(line, (128, 128)).T
        row_at = pl.multiple_of(a * tile, tile)
        line_x = row_ref[0:1, pl.ds(row_at, tile)] * LOG2E
        line_y = row_ref[1:2, pl.ds(row_at, tile)] * LOG2E

        def body(k, carry):
            at = pl.multiple_of(k * step, step)
            col_x = wide_x[pl.ds(at, step), :]
            col_y = wide_y[pl.ds(at, step), :]
            for part in range(tile // 128):
                lanes = slice(part * 128, (part + 1) * 128)
                dx = col_x - line_x[:, lanes]
                dy = col_y - line_y[:, lanes]
                square = dx * dx + dy * dy
                dist = square * lax.rsqrt(jnp.maximum(square, 1e-35))
                block[slot, pl.ds(at, step), lanes] = jnp.exp2(-dist).astype(jnp.bfloat16)
            return carry

        lax.fori_loop(0, tile // step, body, 0)
        store(index).start()
        return carry

    lax.fori_loop(0, count, make_tile, 0)
    for back in (2, 1):

        @pl.when(count >= back)
        def _(back=back):
            store(count - back).wait()


def dense_tiles(near, row_coords, col_coords, rows_local, cols_local, tile):
    return pl.pallas_call(
        dense_kernel,
        out_shape=jax.ShapeDtypeStruct((rows_local, cols_local, tile, tile), jnp.bfloat16),
        in_specs=[
            pl.BlockSpec(memory_space=SMEM),
            pl.BlockSpec(memory_space=VMEM),
            pl.BlockSpec(memory_space=HBM),
        ],
        out_specs=pl.BlockSpec(memory_space=HBM),
        scratch_shapes=[
            pltpu.VMEM((2, cols_local * tile), jnp.float32),
            pltpu.VMEM((tile, 128), jnp.float32),
            pltpu.VMEM((tile, 128), jnp.float32),
            pltpu.VMEM((2, tile, tile), jnp.bfloat16),
            pltpu.SMEM((rows_local * cols_local + 1,), jnp.int32),
            pltpu.SemaphoreType.DMA,
            pltpu.SemaphoreType.DMA((2,)),
        ],
        compiler_params=pltpu.CompilerParams(vmem_limit_bytes=52 << 20),
        cost_estimate=pl.CostEstimate(flops=20_000_000, bytes_accessed=16_000_000, transcendentals=16_000_000),
        name="dense_tiles",
    )(near, row_coords, col_coords)


def apply_kernel(row, near_ref, ranks_ref, draws_ref, v_ref, u_ref, dense_hbm, keep_ref, send_ref, total, dense, sems):
    cols_local, rank, tile = v_ref.shape[1:]
    width = draws_ref.shape[0]
    half = width // 2
    first = first_column(cols_local)
    near = [is_near(near_ref, row, first + b) for b in range(cols_local)]
    fetches = [pltpu.make_async_copy(dense_hbm.at[row, b], dense.at[b], sems.at[b]) for b in range(cols_local)]
    for b in range(cols_local):

        @pl.when(near[b])
        def _(b=b):
            fetches[b].start()

    total[...] = jnp.zeros_like(total)
    for b in range(cols_local):
        lanes = slice(b * tile, (b + 1) * tile)

        @pl.when(near[b])
        def _(b=b, lanes=lanes):
            fetches[b].wait()
            piece = draws_ref[:, lanes]
            for at in range(0, tile, 256):
                part = slice(at, at + 256)
                product = jnp.dot(piece, dense[b, :, part], preferred_element_type=jnp.float32)
                total[:, part] += product * 0.03125

        @pl.when(jnp.logical_not(near[b]))
        def _(b=b, lanes=lanes):
            reduced = lax.dot_general(
                draws_ref[:, lanes], v_ref[row, b], (((1,), (1,)), ((), ())), preferred_element_type=jnp.float32
            )
            ids = lax.broadcasted_iota(jnp.int32, reduced.shape, 1)
            reduced = jnp.where(ids < ranks_ref[row, b], reduced, 0.0).astype(jnp.bfloat16)
            for at in range(0, tile, 256):
                part = slice(at, at + 256)
                total[:, part] += jnp.dot(reduced, u_ref[row, b, :, part], preferred_element_type=jnp.float32)

    core = lax.axis_index("c")
    keep_ref[...] = total[pl.ds(pl.multiple_of(core * half, half), half), :]
    send_ref[...] = total[pl.ds(pl.multiple_of((1 - core) * half, half), half), :]


def apply_row(row, near, ranks, draws, v_factors, u_factors, dense):
    cols_local, _, tile = v_factors.shape[1:]
    width = draws.shape[0]
    half = jax.ShapeDtypeStruct((width // 2, tile), jnp.float32)
    return pl.pallas_call(
        functools.partial(apply_kernel, row),
        out_shape=(half, half),
        in_specs=[pl.BlockSpec(memory_space=SMEM)] * 2
        + [pl.BlockSpec(memory_space=VMEM)] * 3
        + [pl.BlockSpec(memory_space=HBM)],
        out_specs=(pl.BlockSpec(memory_space=VMEM),) * 2,
        scratch_shapes=[
            pltpu.VMEM((width, tile), jnp.float32),
            pltpu.VMEM((cols_local, tile, tile), jnp.bfloat16),
            pltpu.SemaphoreType.DMA((cols_local,)),
        ],
        compiler_params=pltpu.CompilerParams(vmem_limit_bytes=52 << 20),
        cost_estimate=pl.CostEstimate(flops=500_000_000, bytes_accessed=8_000_000, transcendentals=0),
        name="apply_row",
    )(near, ranks, draws, v_factors, u_factors, dense)


def fold_kernel(*refs):
    *parts, out_ref = refs
    rows_local = len(parts) // 2
    tile = parts[0].shape[1]
    for row in range(rows_local):
        both = parts[row][...] + parts[rows_local + row][...]
        for z in range(out_ref.shape[0]):
            block = jnp.concatenate([both[4 * z : 4 * z + 4], both[32 + 4 * z : 36 + 4 * z]], axis=0)
            out_ref[z, :, row * tile : (row + 1) * tile] = block.astype(jnp.bfloat16)


def per_device(draws, u_factors, v_factors, ranks, near, row_coords, col_coords):
    rows_local, cols_local, tile, rank = u_factors.shape
    ny, nx, nz, nc = SIZES
    own = draws.shape[0]
    span = draws.shape[1]
    u_t = jnp.swapaxes(u_factors, 2, 3)
    v_t = jnp.swapaxes(v_factors, 2, 3)
    dense = dense_tiles(near, row_coords, col_coords, rows_local, cols_local, tile)
    column = lax.all_to_all(jnp.broadcast_to(draws[None], (ny, own, span)), "y", 0, 0)
    column = column.reshape(ny * own, span)
    plane = lax.all_to_all(jnp.broadcast_to(column[None], (nx, ny * own, span)), "x", 0, 0)
    plane = plane.reshape(nx * ny * own, span)
    keeps, others = [], []
    for row in range(rows_local):
        keep, send = apply_row(row, near, ranks, plane, v_t, u_t, dense)
        keeps.append(keep)
        pairs = [(i, i ^ 1) for i in range(nz * nc)]
        others.append(lax.ppermute(send, ("z", "c"), pairs))
    blocks = pl.pallas_call(
        fold_kernel,
        out_shape=jax.ShapeDtypeStruct((nz, 8, rows_local * tile), jnp.bfloat16),
        compiler_params=pltpu.CompilerParams(vmem_limit_bytes=6 << 20),
        name="fold",
    )(*keeps, *others)
    spread = lax.all_to_all(blocks, "z", 0, 0)
    return jnp.sum(spread.astype(jnp.float32), axis=0)


def solution(mesh):
    fine = Mesh(mesh.devices.reshape(SIZES), AXES)
    row, col = ("y", "x"), ("z", "c")
    return jax.shard_map(
        per_device,
        mesh=fine,
        in_specs=(
            P(row, col),
            P(row, col, None, None),
            P(row, col, None, None),
            P(row, col),
            P(row, None),
            P(None, row),
            P(),
        ),
        out_specs=P(col, row),
        check_vma=False,
    )
```

```python
import functools

import jax
import jax.numpy as jnp
from jax import lax
from jax.experimental import pallas as pl
from jax.experimental.pallas import tpu as pltpu
from jax.sharding import Mesh, PartitionSpec as P

LOG2E = 1.4426950408889634
AXES = ("y", "x", "z", "c")
SIZES = (8, 4, 8, 2)
VMEM = pltpu.MemorySpace.VMEM
SMEM = pltpu.MemorySpace.SMEM
HBM = pltpu.MemorySpace.HBM


def first_column(cols_local):
    return (lax.axis_index("z") * 2 + lax.axis_index("c")) * cols_local


def is_near(near_ref, row, column):
    hit = near_ref[row, 0] == column
    for slot in range(1, near_ref.shape[1]):
        hit = jnp.logical_or(hit, near_ref[row, slot] == column)
    return hit


def dense_kernel(a, near_hbm, row_hbm, col_hbm, *refs):
    out_hbm, near_ref, line, coords, wide_x, wide_y, line_x, line_y, block, todo, sems, out_sems = refs[-12:]
    _, cols_local, tile, _ = out_hbm.shape
    first = first_column(cols_local)
    start = pl.multiple_of(first * tile, tile)
    fetches = [
        pltpu.make_async_copy(near_hbm, near_ref, sems.at[0]),
        pltpu.make_async_copy(row_hbm.at[:, pl.ds(a * tile, tile)], line, sems.at[1]),
        pltpu.make_async_copy(col_hbm.at[:, pl.ds(start, cols_local * tile)], coords, sems.at[2]),
    ]
    for fetch in fetches:
        fetch.start()
    fetches[0].wait()
    count = jnp.int32(0)
    for b in range(cols_local):
        todo[count] = b
        count = count + is_near(near_ref, a, first + b).astype(jnp.int32)
    fetches[1].wait()
    fetches[2].wait()
    line_x[...] = jnp.broadcast_to(line[0:1, :] * LOG2E, line_x.shape)
    line_y[...] = jnp.broadcast_to(line[1:2, :] * LOG2E, line_y.shape)
    step = 256

    def store(index):
        slot = lax.rem(index, 2)
        return pltpu.make_async_copy(block.at[slot], out_hbm.at[a, todo[index]], out_sems.at[slot])

    def make_tile(index, carry):
        b, slot = todo[index], lax.rem(index, 2)

        @pl.when(index >= 2)
        def _():
            store(index - 2).wait()

        for part in range(tile // 128):
            at = pl.multiple_of(b * tile + part * 128, 128)
            for axis, wide in ((0, wide_x), (1, wide_y)):
                piece = coords[axis : axis + 1, pl.ds(at, 128)] * LOG2E
                wide[part * 128 : (part + 1) * 128, :] = jnp.broadcast_to(piece, (128, 128)).T

        def body(k, carry):
            at = pl.multiple_of(k * step, step)
            for part in range(tile // 128):
                lanes = slice(part * 128, (part + 1) * 128)
                for q in range(0, step, 16):
                    rows = pl.ds(at + q, 16)
                    dx = wide_x[rows, :] - line_x[:, lanes]
                    dy = wide_y[rows, :] - line_y[:, lanes]
                    square = dx * dx + dy * dy
                    dist = square * lax.rsqrt(jnp.maximum(square, 1e-35))
                    block[slot, rows, lanes] = jnp.exp2(-dist).astype(jnp.bfloat16)
            return carry

        lax.fori_loop(0, tile // step, body, 0)
        store(index).start()
        return carry

    lax.fori_loop(0, count, make_tile, 0)
    for back in (2, 1):

        @pl.when(count >= back)
        def _(back=back):
            store(count - back).wait()


def dense_tiles(a, near, row_coords, col_coords, shape, made=None):
    _, cols_local, tile, _ = shape
    given = [near, row_coords, col_coords] + ([] if made is None else [made])
    return pl.pallas_call(
        functools.partial(dense_kernel, a),
        out_shape=HBM(shape, jnp.bfloat16),
        in_specs=[pl.BlockSpec(memory_space=HBM)] * len(given),
        out_specs=pl.BlockSpec(memory_space=HBM),
        input_output_aliases={} if made is None else {3: 0},
        scratch_shapes=[
            pltpu.SMEM(near.shape, jnp.int32),
            pltpu.VMEM((2, tile), jnp.float32),
            pltpu.VMEM((2, cols_local * tile), jnp.float32),
            pltpu.VMEM((tile, 128), jnp.float32),
            pltpu.VMEM((tile, 128), jnp.float32),
            pltpu.VMEM((16, tile), jnp.float32),
            pltpu.VMEM((16, tile), jnp.float32),
            pltpu.VMEM((2, tile, tile), jnp.bfloat16),
            pltpu.SMEM((cols_local + 1,), jnp.int32),
            pltpu.SemaphoreType.DMA((3,)),
            pltpu.SemaphoreType.DMA((2,)),
        ],
        compiler_params=pltpu.CompilerParams(vmem_limit_bytes=12 << 20),
        cost_estimate=pl.CostEstimate(flops=10_000_000, bytes_accessed=8_000_000, transcendentals=8_000_000),
        name="dense_tiles",
    )(*[pltpu.with_memory_space_constraint(g, HBM) for g in given])


def apply_kernel(near_ref, ranks_ref, draws_ref, v_ref, u_ref, dense_hbm, keep_ref, send_ref, total, dense, reduced, sems):
    rows_local, cols_local, rank, tile = v_ref.shape
    half = draws_ref.shape[0] // 2
    first = first_column(cols_local)
    tiles = [(a, b) for b in range(cols_local) for a in range(rows_local)]
    near = {(a, b): is_near(near_ref, a, first + b) for a, b in tiles}
    fetches = {
        (a, b): pltpu.make_async_copy(
            dense_hbm.at[a, b], dense.at[a * cols_local + b], sems.at[a * cols_local + b]
        )
        for a, b in tiles
    }
    for key in tiles:

        @pl.when(near[key])
        def _(key=key):
            fetches[key].start()

    for b in range(cols_local):
        lanes = slice(b * tile, (b + 1) * tile)
        both = jnp.concatenate([v_ref[a, b] for a in range(rows_local)], axis=0)
        sums = lax.dot_general(
            draws_ref[:, lanes], both, (((1,), (1,)), ((), ())), preferred_element_type=jnp.float32
        )
        ids = lax.broadcasted_iota(jnp.int32, sums.shape, 1)
        limit = jnp.int32(0)
        for a in reversed(range(rows_local)):
            end = a * rank + jnp.where(near[a, b], 0, ranks_ref[a, b])
            limit = jnp.where(ids < (a + 1) * rank, end, limit)
        sums = jnp.where(ids < limit, sums, 0.0).astype(jnp.bfloat16)
        for a in range(rows_local):
            reduced[a, :, b * rank : (b + 1) * rank] = sums[:, a * rank : (a + 1) * rank]
    for a in range(rows_local):
        for at in range(0, tile, 256):
            part = slice(at, at + 256)
            left = u_ref[a, :, :, part].reshape(cols_local * rank, 256)
            total[:, a * tile + at : a * tile + at + 256] = jnp.dot(
                reduced[a], left, preferred_element_type=jnp.float32
            )
    for a, b in tiles:

        @pl.when(near[a, b])
        def _(a=a, b=b):
            fetches[a, b].wait()
            piece = draws_ref[:, b * tile : (b + 1) * tile]
            for at in range(0, tile, 256):
                product = jnp.dot(
                    piece, dense[a * cols_local + b, :, at : at + 256], preferred_element_type=jnp.float32
                )
                total[:, a * tile + at : a * tile + at + 256] += product * 0.03125

    core = lax.axis_index("c")
    keep_ref[...] = total[pl.ds(pl.multiple_of(core * half, half), half), :]
    send_ref[...] = total[pl.ds(pl.multiple_of((1 - core) * half, half), half), :]


def apply_tiles(near, ranks, draws, v_factors, u_factors, dense):
    rows_local, cols_local, rank, tile = v_factors.shape
    width = draws.shape[0]
    half = jax.ShapeDtypeStruct((width // 2, rows_local * tile), jnp.float32)
    count = rows_local * cols_local
    return pl.pallas_call(
        apply_kernel,
        out_shape=(half, half),
        in_specs=[pl.BlockSpec(memory_space=SMEM)] * 2
        + [pl.BlockSpec(memory_space=VMEM)] * 3
        + [pl.BlockSpec(memory_space=HBM)],
        out_specs=(pl.BlockSpec(memory_space=VMEM),) * 2,
        scratch_shapes=[
            pltpu.VMEM((width, rows_local * tile), jnp.float32),
            pltpu.VMEM((count, tile, tile), jnp.bfloat16),
            pltpu.VMEM((rows_local, width, cols_local * rank), jnp.bfloat16),
            pltpu.SemaphoreType.DMA((count,)),
        ],
        compiler_params=pltpu.CompilerParams(vmem_limit_bytes=32 << 20),
        cost_estimate=pl.CostEstimate(flops=1_000_000_000, bytes_accessed=16_000_000, transcendentals=0),
        name="apply_tiles",
    )(near, ranks, draws, v_factors, u_factors, pltpu.with_memory_space_constraint(dense, HBM))


def fold_kernel(keep_ref, other_ref, out_ref):
    both = keep_ref[...] + other_ref[...]
    for z in range(out_ref.shape[0]):
        block = jnp.concatenate([both[4 * z : 4 * z + 4], both[32 + 4 * z : 36 + 4 * z]], axis=0)
        out_ref[z] = block.astype(jnp.bfloat16)


def per_device(draws, u_factors, v_factors, ranks, near, row_coords, col_coords):
    rows_local, cols_local, tile, rank = u_factors.shape
    ny, nx, nz, nc = SIZES
    own = draws.shape[0]
    span = draws.shape[1]
    u_t = jnp.swapaxes(u_factors, 2, 3)
    v_t = jnp.swapaxes(v_factors, 2, 3)
    shape = (rows_local, cols_local, tile, tile)
    column = lax.all_to_all(jnp.broadcast_to(draws[None], (ny, own, span)), "y", 0, 0)
    dense = dense_tiles(0, near, row_coords, col_coords, shape)
    column, dense, late = lax.optimization_barrier((column, dense, near))
    column = column.reshape(ny * own, span)
    plane = lax.all_to_all(jnp.broadcast_to(column[None], (nx, ny * own, span)), "x", 0, 0)
    dense = dense_tiles(1, late, row_coords, col_coords, shape, dense)
    plane = plane.reshape(nx * ny * own, span)
    keep, send = apply_tiles(near, ranks, plane, v_t, u_t, dense)
    pairs = [(i, i ^ 1) for i in range(nz * nc)]
    other = lax.ppermute(send, ("z", "c"), pairs)
    blocks = pl.pallas_call(
        fold_kernel,
        out_shape=jax.ShapeDtypeStruct((nz, 8, rows_local * tile), jnp.bfloat16),
        compiler_params=pltpu.CompilerParams(vmem_limit_bytes=6 << 20),
        name="fold",
    )(keep, other)
    spread = lax.all_to_all(blocks, "z", 0, 0)
    return jnp.sum(spread.astype(jnp.float32), axis=0)


def solution(mesh):
    fine = Mesh(mesh.devices.reshape(SIZES), AXES)
    row, col = ("y", "x"), ("z", "c")
    return jax.shard_map(
        per_device,
        mesh=fine,
        in_specs=(
            P(row, col),
            P(row, col, None, None),
            P(row, col, None, None),
            P(row, col),
            P(row, None),
            P(None, row),
            P(),
        ),
        out_specs=P(col, row),
        check_vma=False,
    )
```

```python
import functools

import jax
import jax.numpy as jnp
import numpy as np
from jax import lax
from jax.experimental import pallas as pl
from jax.experimental.pallas import tpu as pltpu
from jax.sharding import Mesh, PartitionSpec as P

LOG2E = 1.4426950408889634
AXES = ("y", "x", "z", "c")
SIZES = (8, 4, 8, 2)
VMEM = pltpu.MemorySpace.VMEM
SMEM = pltpu.MemorySpace.SMEM
HBM = pltpu.MemorySpace.HBM


Y_ORDER = (0, 4, 2, 6, 1, 5, 3, 7)
Z_ORDER = (0, 3, 6, 1, 4, 7, 2, 5)
X_ORDER = (0, 1, 2, 3)


def orders(order):
    return order, order[::-1]


def partners(axis, order):
    ids = np.arange(np.prod(SIZES)).reshape(SIZES)
    lines = np.moveaxis(ids, AXES.index(axis), -1)
    groups = []
    for core, places in enumerate(orders(order)):
        one = lines[..., core, :] if axis != "c" else lines
        groups += one[..., list(places)].reshape(-1, len(order)).tolist()
    return groups


def first_column(cols_local):
    return (lax.axis_index("z") * 2 + lax.axis_index("c")) * cols_local


def is_near(near_ref, row, column):
    hit = near_ref[row, 0] == column
    for slot in range(1, near_ref.shape[1]):
        hit = jnp.logical_or(hit, near_ref[row, slot] == column)
    return hit


def dense_kernel(low, high, near_hbm, row_hbm, col_hbm, *refs):
    out_hbm, near_ref, lines, coords, wide_x, wide_y, line_x, line_y, block, todo, sems, out_sems = refs[-12:]
    rows_local, cols_local, tile, _ = out_hbm.shape
    first = first_column(cols_local)
    start = pl.multiple_of(first * tile, tile)
    fetches = [
        pltpu.make_async_copy(near_hbm, near_ref, sems.at[0]),
        pltpu.make_async_copy(row_hbm, lines, sems.at[1]),
        pltpu.make_async_copy(col_hbm.at[:, pl.ds(start, cols_local * tile)], coords, sems.at[2]),
    ]
    for fetch in fetches:
        fetch.start()
    fetches[0].wait()
    count = jnp.int32(0)
    for b in range(cols_local):
        for a in range(rows_local):
            todo[count] = b * rows_local + a
            count = count + is_near(near_ref, a, first + b).astype(jnp.int32)
    fetches[1].wait()
    fetches[2].wait()
    begin, end = jnp.minimum(count, low), jnp.minimum(count, high)
    step = 256

    @pl.when(begin < end)
    def _():
        for a in range(rows_local):
            lanes = slice(a * tile, (a + 1) * tile)
            line_x[a] = jnp.broadcast_to(lines[0:1, lanes] * LOG2E, line_x.shape[1:])
            line_y[a] = jnp.broadcast_to(lines[1:2, lanes] * LOG2E, line_y.shape[1:])

    def place(index):
        return lax.rem(todo[index], rows_local), lax.div(todo[index], rows_local), lax.rem(index, 2)

    def store(index, at=0, size=tile):
        a, b, slot = place(index)
        rows = pl.ds(at, size)
        return pltpu.make_async_copy(block.at[slot, rows], out_hbm.at[a, b, rows], out_sems.at[slot])

    def make_tile(index, carry):
        a, b, slot = place(index)

        @pl.when(index >= begin + 2)
        def _():
            store(index - 2).wait()

        @pl.when(jnp.logical_or(index == begin, b != place(jnp.maximum(index - 1, 0))[1]))
        def _():
            for part in range(tile // 128):
                at = pl.multiple_of(b * tile + part * 128, 128)
                for axis, wide in ((0, wide_x), (1, wide_y)):
                    piece = coords[axis : axis + 1, pl.ds(at, 128)] * LOG2E
                    wide[part * 128 : (part + 1) * 128, :] = jnp.broadcast_to(piece, (128, 128)).T

        def body(k, carry):
            at = pl.multiple_of(k * step, step)
            for part in range(tile // 128):
                lanes = slice(part * 128, (part + 1) * 128)
                for q in range(0, step, 16):
                    rows = pl.ds(at + q, 16)
                    dx = wide_x[rows, :] - line_x[a, :, lanes]
                    dy = wide_y[rows, :] - line_y[a, :, lanes]
                    square = dx * dx + dy * dy
                    dist = square * lax.rsqrt(jnp.maximum(square, 1e-35))
                    block[slot, rows, lanes] = jnp.exp2(-dist).astype(jnp.bfloat16)
            store(index, at, step).start()
            return carry

        lax.fori_loop(0, tile // step, body, 0)
        return carry

    lax.fori_loop(begin, end, make_tile, 0)
    for back in (2, 1):

        @pl.when(end - begin >= back)
        def _(back=back):
            store(end - back).wait()


def dense_tiles(low, high, near, row_coords, col_coords, shape, made=None):
    rows_local, cols_local, tile, _ = shape
    given = [near, row_coords, col_coords] + ([] if made is None else [made])
    return pl.pallas_call(
        functools.partial(dense_kernel, low, high),
        out_shape=HBM(shape, jnp.bfloat16),
        in_specs=[pl.BlockSpec(memory_space=HBM)] * len(given),
        out_specs=pl.BlockSpec(memory_space=HBM),
        input_output_aliases={} if made is None else {3: 0},
        scratch_shapes=[
            pltpu.SMEM(near.shape, jnp.int32),
            pltpu.VMEM(row_coords.shape, jnp.float32),
            pltpu.VMEM((2, cols_local * tile), jnp.float32),
            pltpu.VMEM((tile, 128), jnp.float32),
            pltpu.VMEM((tile, 128), jnp.float32),
            pltpu.VMEM((rows_local, 16, tile), jnp.float32),
            pltpu.VMEM((rows_local, 16, tile), jnp.float32),
            pltpu.VMEM((2, tile, tile), jnp.bfloat16),
            pltpu.SMEM((rows_local * cols_local + 1,), jnp.int32),
            pltpu.SemaphoreType.DMA((3,)),
            pltpu.SemaphoreType.DMA((2,)),
        ],
        compiler_params=pltpu.CompilerParams(vmem_limit_bytes=12 << 20),
        cost_estimate=pl.CostEstimate(flops=10_000_000, bytes_accessed=8_000_000, transcendentals=8_000_000),
        name="dense_tiles",
    )(*[pltpu.with_memory_space_constraint(g, HBM) for g in given])


def apply_kernel(near_ref, ranks_ref, draws_ref, v_ref, u_ref, dense_hbm, keep_ref, send_ref, total, dense, reduced, sems):
    rows_local, cols_local, rank, tile = v_ref.shape
    half = draws_ref.shape[0] // 2
    first = first_column(cols_local)
    tiles = [(a, b) for b in range(cols_local) for a in range(rows_local)]
    near = {}
    fetches = {
        (a, b): pltpu.make_async_copy(
            dense_hbm.at[a, b], dense.at[a * cols_local + b], sems.at[a * cols_local + b]
        )
        for a, b in tiles
    }
    for key in tiles:
        near[key] = is_near(near_ref, key[0], first + key[1])

        @pl.when(near[key])
        def _(key=key):
            fetches[key].start()

    for b in range(cols_local):
        lanes = slice(b * tile, (b + 1) * tile)
        both = jnp.concatenate([v_ref[a, b] for a in range(rows_local)], axis=0)
        sums = lax.dot_general(
            draws_ref[:, lanes], both, (((1,), (1,)), ((), ())), preferred_element_type=jnp.float32
        )
        ids = lax.broadcasted_iota(jnp.int32, sums.shape, 1)
        limit = jnp.int32(0)
        for a in reversed(range(rows_local)):
            end = a * rank + jnp.where(near[a, b], 0, ranks_ref[a, b])
            limit = jnp.where(ids < (a + 1) * rank, end, limit)
        sums = jnp.where(ids < limit, sums, 0.0).astype(jnp.bfloat16)
        for a in range(rows_local):
            reduced[a, :, b * rank : (b + 1) * rank] = sums[:, a * rank : (a + 1) * rank]
    for a in range(rows_local):
        for at in range(0, tile, 256):
            part = slice(at, at + 256)
            left = u_ref[a, :, :, part].reshape(cols_local * rank, 256)
            total[:, a * tile + at : a * tile + at + 256] = jnp.dot(
                reduced[a], left, preferred_element_type=jnp.float32
            )
    for a, b in tiles:

        @pl.when(near[a, b])
        def _(a=a, b=b):
            fetches[a, b].wait()
            piece = draws_ref[:, b * tile : (b + 1) * tile]
            for at in range(0, tile, 256):
                product = jnp.dot(
                    piece, dense[a * cols_local + b, :, at : at + 256], preferred_element_type=jnp.float32
                )
                total[:, a * tile + at : a * tile + at + 256] += product * 0.03125

    keep_ref[...] = total[:half, :]
    send_ref[...] = total[half:, :]


def apply_tiles(near, ranks, draws, v_factors, u_factors, dense):
    rows_local, cols_local, rank, tile = v_factors.shape
    width = draws.shape[0]
    half = jax.ShapeDtypeStruct((width // 2, rows_local * tile), jnp.float32)
    count = rows_local * cols_local
    return pl.pallas_call(
        apply_kernel,
        out_shape=(half, half),
        in_specs=[pl.BlockSpec(memory_space=SMEM)] * 2
        + [pl.BlockSpec(memory_space=VMEM)] * 3
        + [pl.BlockSpec(memory_space=HBM)],
        out_specs=(pl.BlockSpec(memory_space=VMEM),) * 2,
        scratch_shapes=[
            pltpu.VMEM((width, rows_local * tile), jnp.float32),
            pltpu.VMEM((count, tile, tile), jnp.bfloat16),
            pltpu.VMEM((rows_local, width, cols_local * rank), jnp.bfloat16),
            pltpu.SemaphoreType.DMA((count,)),
        ],
        compiler_params=pltpu.CompilerParams(vmem_limit_bytes=32 << 20),
        cost_estimate=pl.CostEstimate(flops=1_000_000_000, bytes_accessed=16_000_000, transcendentals=0),
        name="apply_tiles",
    )(near, ranks, draws, v_factors, u_factors, pltpu.with_memory_space_constraint(dense, HBM))


def fold_kernel(keep_ref, other_ref, out_ref):
    blocks = out_ref.shape[0]
    core = lax.axis_index("c")
    for at in range(blocks):
        back = blocks - 1 - at
        first = keep_ref[4 * at : 4 * at + 4] + other_ref[32 + 4 * back : 36 + 4 * back]
        second = keep_ref[32 + 4 * at : 36 + 4 * at] + other_ref[4 * back : 4 * back + 4]
        lower = jnp.where(core == 0, first, second)
        upper = jnp.where(core == 0, second, first)
        places = [z.index(y[at]) for y, z in zip(orders(Y_ORDER), orders(Z_ORDER))]
        place = jnp.where(core == 0, places[0], places[1])
        out_ref[place] = jnp.concatenate([lower, upper], axis=0).astype(jnp.bfloat16)


def per_device(draws, u_factors, v_factors, ranks, near, row_coords, col_coords):
    rows_local, cols_local, tile, rank = u_factors.shape
    ny, nx, nz, nc = SIZES
    own = draws.shape[0]
    span = draws.shape[1]
    u_t = jnp.swapaxes(u_factors, 2, 3)
    v_t = jnp.swapaxes(v_factors, 2, 3)
    shape = (rows_local, cols_local, tile, tile)
    copies = jnp.broadcast_to(draws[None], (ny, own, span))
    column = lax.all_to_all(copies, AXES, 0, 0, axis_index_groups=partners("y", Y_ORDER))
    dense = dense_tiles(0, 3, near, row_coords, col_coords, shape)
    column, dense, late = lax.optimization_barrier((column, dense, near))
    column = column.reshape(ny * own, span)
    copies = jnp.broadcast_to(column[None], (nx, ny * own, span))
    plane = lax.all_to_all(copies, AXES, 0, 0, axis_index_groups=partners("x", X_ORDER))
    dense = dense_tiles(3, 8, late, row_coords, col_coords, shape, dense)
    plane = plane.reshape(nx * ny * own, span)
    keep, send = apply_tiles(near, ranks, plane, v_t, u_t, dense)
    pairs = [(i, i ^ 1) for i in range(nz * nc)]
    other = lax.ppermute(send, ("z", "c"), pairs)
    blocks = pl.pallas_call(
        fold_kernel,
        out_shape=jax.ShapeDtypeStruct((nz, 8, rows_local * tile), jnp.bfloat16),
        compiler_params=pltpu.CompilerParams(vmem_limit_bytes=6 << 20),
        name="fold",
    )(keep, other)
    spread = lax.all_to_all(blocks, AXES, 0, 0, axis_index_groups=partners("z", Z_ORDER))
    return jnp.sum(spread.astype(jnp.float32), axis=0)


def solution(mesh):
    fine = Mesh(mesh.devices.reshape(SIZES), AXES)
    row, col = ("y", "x"), ("z", "c")
    return jax.shard_map(
        per_device,
        mesh=fine,
        in_specs=(
            P(row, col),
            P(row, col, None, None),
            P(row, col, None, None),
            P(row, col),
            P(row, None),
            P(None, row),
            P(),
        ),
        out_specs=P(col, row),
        check_vma=False,
    )
```

```python
import functools

import jax
import jax.numpy as jnp
import numpy as np
from jax import lax
from jax.experimental import pallas as pl
from jax.experimental.pallas import tpu as pltpu
from jax.sharding import Mesh, PartitionSpec as P

LOG2E = 1.4426950408889634
AXES = ("y", "x", "z", "c")
SIZES = (8, 4, 8, 2)
VMEM = pltpu.MemorySpace.VMEM
SMEM = pltpu.MemorySpace.SMEM
HBM = pltpu.MemorySpace.HBM


Y_ORDER = (0, 4, 2, 6, 1, 5, 3, 7)
Z_ORDER = (6, 2, 7, 3, 1, 5, 0, 4)
X_ORDER = (0, 1, 2, 3)


def orders(order):
    return order, order[::-1]


def partners(axis, order):
    ids = np.arange(np.prod(SIZES)).reshape(SIZES)
    lines = np.moveaxis(ids, AXES.index(axis), -1)
    groups = []
    for core, places in enumerate(orders(order)):
        one = lines[..., core, :] if axis != "c" else lines
        groups += one[..., list(places)].reshape(-1, len(order)).tolist()
    return groups


def first_column(cols_local):
    return (lax.axis_index("z") * 2 + lax.axis_index("c")) * cols_local


def is_near(near_ref, row, column):
    hit = near_ref[row, 0] == column
    for slot in range(1, near_ref.shape[1]):
        hit = jnp.logical_or(hit, near_ref[row, slot] == column)
    return hit


def dense_kernel(low, high, near_hbm, row_hbm, col_hbm, *refs):
    out_hbm, near_ref, lines, coords, wide_x, wide_y, line_x, line_y, block, todo, sems, out_sems = refs[-12:]
    rows_local, cols_local, tile, _ = out_hbm.shape
    first = first_column(cols_local)
    start = pl.multiple_of(first * tile, tile)
    fetches = [
        pltpu.make_async_copy(near_hbm, near_ref, sems.at[0]),
        pltpu.make_async_copy(row_hbm, lines, sems.at[1]),
        pltpu.make_async_copy(col_hbm.at[:, pl.ds(start, cols_local * tile)], coords, sems.at[2]),
    ]
    for fetch in fetches:
        fetch.start()
    fetches[0].wait()
    count = jnp.int32(0)
    for b in range(cols_local):
        for a in range(rows_local):
            todo[count] = b * rows_local + a
            count = count + is_near(near_ref, a, first + b).astype(jnp.int32)
    fetches[1].wait()
    fetches[2].wait()
    begin, end = jnp.minimum(count, low), jnp.minimum(count, high)
    step = 512

    @pl.when(begin < end)
    def _():
        for a in range(rows_local):
            lanes = slice(a * tile, (a + 1) * tile)
            line_x[a] = jnp.broadcast_to(lines[0:1, lanes] * LOG2E, line_x.shape[1:])
            line_y[a] = jnp.broadcast_to(lines[1:2, lanes] * LOG2E, line_y.shape[1:])

    def place(index):
        return lax.rem(todo[index], rows_local), lax.div(todo[index], rows_local), lax.rem(index, 2)

    def store(index, at=0, size=tile):
        a, b, slot = place(index)
        rows = pl.ds(at, size)
        return pltpu.make_async_copy(block.at[slot, rows], out_hbm.at[a, b, rows], out_sems.at[slot])

    def make_tile(index, carry):
        a, b, slot = place(index)

        @pl.when(index >= begin + 2)
        def _():
            store(index - 2).wait()

        @pl.when(jnp.logical_or(index == begin, b != place(jnp.maximum(index - 1, 0))[1]))
        def _():
            for part in range(tile // 128):
                at = pl.multiple_of(b * tile + part * 128, 128)
                for axis, wide in ((0, wide_x), (1, wide_y)):
                    piece = coords[axis : axis + 1, pl.ds(at, 128)] * LOG2E
                    wide[part * 128 : (part + 1) * 128, :] = jnp.broadcast_to(piece, (128, 128)).T

        def body(k, carry):
            at = pl.multiple_of(k * step, step)
            for part in range(tile // 128):
                lanes = slice(part * 128, (part + 1) * 128)
                for q in range(0, step, 16):
                    rows = pl.ds(at + q, 16)
                    dx = wide_x[rows, :] - line_x[a, :, lanes]
                    dy = wide_y[rows, :] - line_y[a, :, lanes]
                    square = dx * dx + dy * dy
                    dist = square * lax.rsqrt(jnp.maximum(square, 1e-35))
                    block[slot, rows, lanes] = jnp.exp2(-dist).astype(jnp.bfloat16)
            store(index, at, step).start()
            return carry

        lax.fori_loop(0, tile // step, body, 0)
        return carry

    lax.fori_loop(begin, end, make_tile, 0)
    for back in (2, 1):

        @pl.when(end - begin >= back)
        def _(back=back):
            store(end - back).wait()


def dense_tiles(low, high, near, row_coords, col_coords, shape, made=None):
    rows_local, cols_local, tile, _ = shape
    given = [near, row_coords, col_coords] + ([] if made is None else [made])
    return pl.pallas_call(
        functools.partial(dense_kernel, low, high),
        out_shape=HBM(shape, jnp.bfloat16),
        in_specs=[pl.BlockSpec(memory_space=HBM)] * len(given),
        out_specs=pl.BlockSpec(memory_space=HBM),
        input_output_aliases={} if made is None else {3: 0},
        scratch_shapes=[
            pltpu.SMEM(near.shape, jnp.int32),
            pltpu.VMEM(row_coords.shape, jnp.float32),
            pltpu.VMEM((2, cols_local * tile), jnp.float32),
            pltpu.VMEM((tile, 128), jnp.float32),
            pltpu.VMEM((tile, 128), jnp.float32),
            pltpu.VMEM((rows_local, 16, tile), jnp.float32),
            pltpu.VMEM((rows_local, 16, tile), jnp.float32),
            pltpu.VMEM((2, tile, tile), jnp.bfloat16),
            pltpu.SMEM((rows_local * cols_local + 1,), jnp.int32),
            pltpu.SemaphoreType.DMA((3,)),
            pltpu.SemaphoreType.DMA((2,)),
        ],
        compiler_params=pltpu.CompilerParams(vmem_limit_bytes=12 << 20),
        cost_estimate=pl.CostEstimate(flops=10_000_000, bytes_accessed=8_000_000, transcendentals=8_000_000),
        name="dense_tiles",
    )(*[pltpu.with_memory_space_constraint(g, HBM) for g in given])


def apply_kernel(near_ref, ranks_ref, draws_ref, v_ref, u_ref, dense_hbm, keep_ref, send_ref, dense, reduced, sems):
    rows_local, cols_local, rank, tile = v_ref.shape
    half = draws_ref.shape[0] // 2
    first = first_column(cols_local)
    tiles = [(a, b) for b in range(cols_local) for a in range(rows_local)]
    near = {}
    fetches = {
        (a, b): pltpu.make_async_copy(
            dense_hbm.at[a, b], dense.at[a * cols_local + b], sems.at[a * cols_local + b]
        )
        for a, b in tiles
    }
    for key in tiles:
        near[key] = is_near(near_ref, key[0], first + key[1])

        @pl.when(near[key])
        def _(key=key):
            fetches[key].start()

    for b in range(cols_local):
        lanes = slice(b * tile, (b + 1) * tile)
        both = jnp.concatenate([v_ref[a, b] for a in range(rows_local)], axis=0)
        sums = lax.dot_general(
            draws_ref[:, lanes], both, (((1,), (1,)), ((), ())), preferred_element_type=jnp.float32
        )
        ids = lax.broadcasted_iota(jnp.int32, sums.shape, 1)
        limit = jnp.int32(0)
        for a in reversed(range(rows_local)):
            end = a * rank + jnp.where(near[a, b], 0, ranks_ref[a, b])
            limit = jnp.where(ids < (a + 1) * rank, end, limit)
        sums = jnp.where(ids < limit, sums, 0.0).astype(jnp.bfloat16)
        for a in range(rows_local):
            reduced[a, :, b * rank : (b + 1) * rank] = sums[:, a * rank : (a + 1) * rank]
    for a in range(rows_local):
        for at in range(0, tile, 256):
            part = slice(at, at + 256)
            left = u_ref[a, :, :, part].reshape(cols_local * rank, 256)
            lanes = slice(a * tile + at, a * tile + at + 256)
            product = jnp.dot(reduced[a], left, preferred_element_type=jnp.float32)
            keep_ref[:, lanes] = product[:half]
            send_ref[:, lanes] = product[half:]
    for a, b in tiles:

        @pl.when(near[a, b])
        def _(a=a, b=b):
            fetches[a, b].wait()
            piece = draws_ref[:, b * tile : (b + 1) * tile]
            for at in range(0, tile, 256):
                product = jnp.dot(
                    piece, dense[a * cols_local + b, :, at : at + 256], preferred_element_type=jnp.float32
                )
                lanes = slice(a * tile + at, a * tile + at + 256)
                keep_ref[:, lanes] += product[:half] * 0.03125
                send_ref[:, lanes] += product[half:] * 0.03125


def apply_tiles(near, ranks, draws, v_factors, u_factors, dense):
    rows_local, cols_local, rank, tile = v_factors.shape
    width = draws.shape[0]
    half = jax.ShapeDtypeStruct((width // 2, rows_local * tile), jnp.float32)
    count = rows_local * cols_local
    return pl.pallas_call(
        apply_kernel,
        out_shape=(half, half),
        in_specs=[pl.BlockSpec(memory_space=SMEM)] * 2
        + [pl.BlockSpec(memory_space=VMEM)] * 3
        + [pl.BlockSpec(memory_space=HBM)],
        out_specs=(pl.BlockSpec(memory_space=VMEM),) * 2,
        scratch_shapes=[
            pltpu.VMEM((count, tile, tile), jnp.bfloat16),
            pltpu.VMEM((rows_local, width, cols_local * rank), jnp.bfloat16),
            pltpu.SemaphoreType.DMA((count,)),
        ],
        compiler_params=pltpu.CompilerParams(vmem_limit_bytes=32 << 20),
        cost_estimate=pl.CostEstimate(flops=1_000_000_000, bytes_accessed=16_000_000, transcendentals=0),
        name="apply_tiles",
    )(near, ranks, draws, v_factors, u_factors, pltpu.with_memory_space_constraint(dense, HBM))


def fold_kernel(keep_ref, other_ref, out_ref):
    blocks = out_ref.shape[0]
    core = lax.axis_index("c")
    for at in range(blocks):
        back = blocks - 1 - at
        first = keep_ref[4 * at : 4 * at + 4] + other_ref[32 + 4 * back : 36 + 4 * back]
        second = keep_ref[32 + 4 * at : 36 + 4 * at] + other_ref[4 * back : 4 * back + 4]
        lower = jnp.where(core == 0, first, second)
        upper = jnp.where(core == 0, second, first)
        places = [z.index(y[at]) for y, z in zip(orders(Y_ORDER), orders(Z_ORDER))]
        place = jnp.where(core == 0, places[0], places[1])
        out_ref[place] = jnp.concatenate([lower, upper], axis=0).astype(jnp.bfloat16)


def per_device(draws, u_factors, v_factors, ranks, near, row_coords, col_coords):
    rows_local, cols_local, tile, rank = u_factors.shape
    ny, nx, nz, nc = SIZES
    own = draws.shape[0]
    span = draws.shape[1]
    u_t = jnp.swapaxes(u_factors, 2, 3)
    v_t = jnp.swapaxes(v_factors, 2, 3)
    shape = (rows_local, cols_local, tile, tile)
    copies = jnp.broadcast_to(draws[None], (ny, own, span))
    column = lax.all_to_all(copies, AXES, 0, 0, axis_index_groups=partners("y", Y_ORDER))
    dense = dense_tiles(0, 3, near, row_coords, col_coords, shape)
    column, dense, late = lax.optimization_barrier((column, dense, near))
    column = column.reshape(ny * own, span)
    copies = jnp.broadcast_to(column[None], (nx, ny * own, span))
    plane = lax.all_to_all(copies, AXES, 0, 0, axis_index_groups=partners("x", X_ORDER))
    dense = dense_tiles(3, 8, late, row_coords, col_coords, shape, dense)
    plane = plane.reshape(nx * ny * own, span)
    keep, send = apply_tiles(near, ranks, plane, v_t, u_t, dense)
    pairs = [(i, i ^ 1) for i in range(nz * nc)]
    other = lax.ppermute(send, ("z", "c"), pairs)
    blocks = pl.pallas_call(
        fold_kernel,
        out_shape=jax.ShapeDtypeStruct((nz, 8, rows_local * tile), jnp.bfloat16),
        compiler_params=pltpu.CompilerParams(vmem_limit_bytes=6 << 20),
        name="fold",
    )(keep, other)
    spread = lax.all_to_all(blocks, AXES, 0, 0, axis_index_groups=partners("z", Z_ORDER))
    return jnp.sum(spread.astype(jnp.float32), axis=0)


def solution(mesh):
    fine = Mesh(mesh.devices.reshape(SIZES), AXES)
    row, col = ("y", "x"), ("z", "c")
    return jax.shard_map(
        per_device,
        mesh=fine,
        in_specs=(
            P(row, col),
            P(row, col, None, None),
            P(row, col, None, None),
            P(row, col),
            P(row, None),
            P(None, row),
            P(),
        ),
        out_specs=P(col, row),
        check_vma=False,
    )
```

```python
import functools

import jax
import jax.numpy as jnp
import numpy as np
from jax import lax
from jax.experimental import pallas as pl
from jax.experimental.pallas import tpu as pltpu
from jax.sharding import Mesh, PartitionSpec as P

LOG2E = 1.4426950408889634
AXES = ("y", "x", "z", "c")
SIZES = (8, 4, 8, 2)
VMEM = pltpu.MemorySpace.VMEM
SMEM = pltpu.MemorySpace.SMEM
HBM = pltpu.MemorySpace.HBM


Y_ORDER = (0, 4, 2, 6, 1, 5, 3, 7)
Z_ORDER = (3, 7, 2, 6, 4, 0, 5, 1)
X_ORDER = (0, 1, 2, 3)


def orders(order):
    return order, order[::-1]


def partners(axis, order):
    ids = np.arange(np.prod(SIZES)).reshape(SIZES)
    lines = np.moveaxis(ids, AXES.index(axis), -1)
    groups = []
    for core, places in enumerate(orders(order)):
        one = lines[..., core, :] if axis != "c" else lines
        groups += one[..., list(places)].reshape(-1, len(order)).tolist()
    return groups


def first_column(cols_local):
    return (lax.axis_index("z") * 2 + lax.axis_index("c")) * cols_local


def is_near(near_ref, row, column):
    hit = near_ref[row, 0] == column
    for slot in range(1, near_ref.shape[1]):
        hit = jnp.logical_or(hit, near_ref[row, slot] == column)
    return hit


def dense_kernel(low, high, near_hbm, row_hbm, col_hbm, *refs):
    out_hbm, near_ref, lines, coords, wide_x, wide_y, line_x, line_y, block, todo, sems, out_sems = refs[-12:]
    rows_local, cols_local, tile, _ = out_hbm.shape
    first = first_column(cols_local)
    start = pl.multiple_of(first * tile, tile)
    fetches = [
        pltpu.make_async_copy(near_hbm, near_ref, sems.at[0]),
        pltpu.make_async_copy(row_hbm, lines, sems.at[1]),
        pltpu.make_async_copy(col_hbm.at[:, pl.ds(start, cols_local * tile)], coords, sems.at[2]),
    ]
    for fetch in fetches:
        fetch.start()
    fetches[0].wait()
    count = jnp.int32(0)
    for b in range(cols_local):
        for a in range(rows_local):
            todo[count] = b * rows_local + a
            count = count + is_near(near_ref, a, first + b).astype(jnp.int32)
    fetches[1].wait()
    fetches[2].wait()
    begin, end = jnp.minimum(count, low), jnp.minimum(count, high)
    step = 512

    @pl.when(begin < end)
    def _():
        for a in range(rows_local):
            lanes = slice(a * tile, (a + 1) * tile)
            line_x[a] = jnp.broadcast_to(lines[0:1, lanes] * LOG2E, line_x.shape[1:])
            line_y[a] = jnp.broadcast_to(lines[1:2, lanes] * LOG2E, line_y.shape[1:])

    def place(index):
        return lax.rem(todo[index], rows_local), lax.div(todo[index], rows_local), lax.rem(index, 2)

    def store(index, at=0, size=tile):
        a, b, slot = place(index)
        rows = pl.ds(at, size)
        return pltpu.make_async_copy(block.at[slot, rows], out_hbm.at[a, b, rows], out_sems.at[slot])

    def make_tile(index, carry):
        a, b, slot = place(index)

        @pl.when(index >= begin + 2)
        def _():
            store(index - 2).wait()

        @pl.when(jnp.logical_or(index == begin, b != place(jnp.maximum(index - 1, 0))[1]))
        def _():
            for part in range(tile // 128):
                at = pl.multiple_of(b * tile + part * 128, 128)
                for axis, wide in ((0, wide_x), (1, wide_y)):
                    piece = coords[axis : axis + 1, pl.ds(at, 128)] * LOG2E
                    wide[part * 128 : (part + 1) * 128, :] = jnp.broadcast_to(piece, (128, 128)).T

        def body(k, carry):
            at = pl.multiple_of(k * step, step)
            for part in range(tile // 128):
                lanes = slice(part * 128, (part + 1) * 128)
                for q in range(0, step, 16):
                    rows = pl.ds(at + q, 16)
                    dx = wide_x[rows, :] - line_x[a, :, lanes]
                    dy = wide_y[rows, :] - line_y[a, :, lanes]
                    square = dx * dx + dy * dy
                    dist = square * lax.rsqrt(jnp.maximum(square, 1e-35))
                    block[slot, rows, lanes] = jnp.exp2(-dist).astype(jnp.bfloat16)
            store(index, at, step).start()
            return carry

        lax.fori_loop(0, tile // step, body, 0)
        return carry

    lax.fori_loop(begin, end, make_tile, 0)
    for back in (2, 1):

        @pl.when(end - begin >= back)
        def _(back=back):
            store(end - back).wait()


def dense_tiles(low, high, near, row_coords, col_coords, shape, made=None):
    rows_local, cols_local, tile, _ = shape
    given = [near, row_coords, col_coords] + ([] if made is None else [made])
    return pl.pallas_call(
        functools.partial(dense_kernel, low, high),
        out_shape=HBM(shape, jnp.bfloat16),
        in_specs=[pl.BlockSpec(memory_space=HBM)] * len(given),
        out_specs=pl.BlockSpec(memory_space=HBM),
        input_output_aliases={} if made is None else {3: 0},
        scratch_shapes=[
            pltpu.SMEM(near.shape, jnp.int32),
            pltpu.VMEM(row_coords.shape, jnp.float32),
            pltpu.VMEM((2, cols_local * tile), jnp.float32),
            pltpu.VMEM((tile, 128), jnp.float32),
            pltpu.VMEM((tile, 128), jnp.float32),
            pltpu.VMEM((rows_local, 16, tile), jnp.float32),
            pltpu.VMEM((rows_local, 16, tile), jnp.float32),
            pltpu.VMEM((2, tile, tile), jnp.bfloat16),
            pltpu.SMEM((rows_local * cols_local + 1,), jnp.int32),
            pltpu.SemaphoreType.DMA((3,)),
            pltpu.SemaphoreType.DMA((2,)),
        ],
        compiler_params=pltpu.CompilerParams(vmem_limit_bytes=12 << 20),
        cost_estimate=pl.CostEstimate(flops=10_000_000, bytes_accessed=8_000_000, transcendentals=8_000_000),
        name="dense_tiles",
    )(*[pltpu.with_memory_space_constraint(g, HBM) for g in given])


def apply_kernel(near_ref, ranks_ref, draws_ref, v_ref, u_ref, dense_hbm, keep_ref, send_ref, dense, reduced, sems):
    rows_local, cols_local, rank, tile = v_ref.shape
    half = draws_ref.shape[0] // 2
    first = first_column(cols_local)
    tiles = [(a, b) for b in range(cols_local) for a in range(rows_local)]
    near = {}
    fetches = {
        (a, b): pltpu.make_async_copy(
            dense_hbm.at[a, b], dense.at[a * cols_local + b], sems.at[a * cols_local + b]
        )
        for a, b in tiles
    }
    for key in tiles:
        near[key] = is_near(near_ref, key[0], first + key[1])

        @pl.when(near[key])
        def _(key=key):
            fetches[key].start()

    for b in range(cols_local):
        lanes = slice(b * tile, (b + 1) * tile)
        both = jnp.concatenate([v_ref[a, b] for a in range(rows_local)], axis=0)
        sums = lax.dot_general(
            draws_ref[:, lanes], both, (((1,), (1,)), ((), ())), preferred_element_type=jnp.float32
        )
        ids = lax.broadcasted_iota(jnp.int32, sums.shape, 1)
        limit = jnp.int32(0)
        for a in reversed(range(rows_local)):
            end = a * rank + jnp.where(near[a, b], 0, ranks_ref[a, b])
            limit = jnp.where(ids < (a + 1) * rank, end, limit)
        sums = jnp.where(ids < limit, sums, 0.0).astype(jnp.bfloat16)
        for a in range(rows_local):
            reduced[a, :, b * rank : (b + 1) * rank] = sums[:, a * rank : (a + 1) * rank]
    for a in range(rows_local):
        for at in range(0, tile, 256):
            part = slice(at, at + 256)
            left = u_ref[a, :, :, part].reshape(cols_local * rank, 256)
            lanes = slice(a * tile + at, a * tile + at + 256)
            product = jnp.dot(reduced[a], left, preferred_element_type=jnp.float32)
            keep_ref[:, lanes] = product[:half]
            send_ref[:, lanes] = product[half:]
    for a, b in tiles:

        @pl.when(near[a, b])
        def _(a=a, b=b):
            fetches[a, b].wait()
            piece = draws_ref[:, b * tile : (b + 1) * tile]
            for at in range(0, tile, 256):
                product = jnp.dot(
                    piece, dense[a * cols_local + b, :, at : at + 256], preferred_element_type=jnp.float32
                )
                lanes = slice(a * tile + at, a * tile + at + 256)
                keep_ref[:, lanes] += product[:half] * 0.03125
                send_ref[:, lanes] += product[half:] * 0.03125


def apply_tiles(near, ranks, draws, v_factors, u_factors, dense):
    rows_local, cols_local, rank, tile = v_factors.shape
    width = draws.shape[0]
    half = jax.ShapeDtypeStruct((width // 2, rows_local * tile), jnp.float32)
    count = rows_local * cols_local
    return pl.pallas_call(
        apply_kernel,
        out_shape=(half, half),
        in_specs=[pl.BlockSpec(memory_space=SMEM)] * 2
        + [pl.BlockSpec(memory_space=VMEM)] * 3
        + [pl.BlockSpec(memory_space=HBM)],
        out_specs=(pl.BlockSpec(memory_space=VMEM),) * 2,
        scratch_shapes=[
            pltpu.VMEM((count, tile, tile), jnp.bfloat16),
            pltpu.VMEM((rows_local, width, cols_local * rank), jnp.bfloat16),
            pltpu.SemaphoreType.DMA((count,)),
        ],
        compiler_params=pltpu.CompilerParams(vmem_limit_bytes=32 << 20),
        cost_estimate=pl.CostEstimate(flops=1_000_000_000, bytes_accessed=16_000_000, transcendentals=0),
        name="apply_tiles",
    )(near, ranks, draws, v_factors, u_factors, pltpu.with_memory_space_constraint(dense, HBM))


def fold_kernel(keep_ref, other_ref, out_ref):
    blocks = out_ref.shape[0]
    core = lax.axis_index("c")
    for at in range(blocks):
        back = blocks - 1 - at
        first = keep_ref[4 * at : 4 * at + 4] + other_ref[32 + 4 * back : 36 + 4 * back]
        second = keep_ref[32 + 4 * at : 36 + 4 * at] + other_ref[4 * back : 4 * back + 4]
        lower = jnp.where(core == 0, first, second)
        upper = jnp.where(core == 0, second, first)
        places = [z.index(y[at]) for y, z in zip(orders(Y_ORDER), orders(Z_ORDER))]
        place = jnp.where(core == 0, places[0], places[1])
        out_ref[place] = jnp.concatenate([lower, upper], axis=0).astype(jnp.bfloat16)


def per_device(draws, u_factors, v_factors, ranks, near, row_coords, col_coords):
    rows_local, cols_local, tile, rank = u_factors.shape
    ny, nx, nz, nc = SIZES
    own = draws.shape[0]
    span = draws.shape[1]
    u_t = jnp.swapaxes(u_factors, 2, 3)
    v_t = jnp.swapaxes(v_factors, 2, 3)
    shape = (rows_local, cols_local, tile, tile)
    copies = jnp.broadcast_to(draws[None], (ny, own, span))
    column = lax.all_to_all(copies, AXES, 0, 0, axis_index_groups=partners("y", Y_ORDER))
    dense = dense_tiles(0, 3, near, row_coords, col_coords, shape)
    column, dense, late = lax.optimization_barrier((column, dense, near))
    column = column.reshape(ny * own, span)
    copies = jnp.broadcast_to(column[None], (nx, ny * own, span))
    plane = lax.all_to_all(copies, AXES, 0, 0, axis_index_groups=partners("x", X_ORDER))
    dense = dense_tiles(3, 8, late, row_coords, col_coords, shape, dense)
    plane = plane.reshape(nx * ny * own, span)
    keep, send = apply_tiles(near, ranks, plane, v_t, u_t, dense)
    pairs = [(i, i ^ 1) for i in range(nz * nc)]
    other = lax.ppermute(send, ("z", "c"), pairs)
    blocks = pl.pallas_call(
        fold_kernel,
        out_shape=jax.ShapeDtypeStruct((nz, 8, rows_local * tile), jnp.bfloat16),
        compiler_params=pltpu.CompilerParams(vmem_limit_bytes=6 << 20),
        name="fold",
    )(keep, other)
    spread = lax.all_to_all(blocks, AXES, 0, 0, axis_index_groups=partners("z", Z_ORDER))
    return jnp.sum(spread.astype(jnp.float32), axis=0)


def solution(mesh):
    fine = Mesh(mesh.devices.reshape(SIZES), AXES)
    row, col = ("y", "x"), ("z", "c")
    return jax.shard_map(
        per_device,
        mesh=fine,
        in_specs=(
            P(row, col),
            P(row, col, None, None),
            P(row, col, None, None),
            P(row, col),
            P(row, None),
            P(None, row),
            P(),
        ),
        out_specs=P(col, row),
        check_vma=False,
    )
```
